32 devices in a mesh: groups: 2 (over y), pool: 4 (over x, core), tp: 4 (over z).
Axes of the slice: x: 2, y: 2, z: 4, core: 2. Of those that a mesh axis runs over, the one named last changes fastest.
Arguments:
- queries: bfloat16 [192, 16384], P(('groups', 'pool', 'tp')), parts along dimension 0, may hold values from -6 to 6
- cached_entries: bfloat16 [192, 512, 512], P(('groups', 'pool', 'tp')), parts along dimension 0, may hold values from -4.5 to 4.5
- new_entry: bfloat16 [192, 512], P(('groups', 'pool', 'tp')), parts along dimension 0, may hold values from -4.5 to 4.5
- lengths: int32 [192], P(('groups', 'pool', 'tp')), parts along dimension 0, may hold values from 2 to 512, as said below
- residual: bfloat16 [192, 7168], P(('groups', 'pool'), 'tp'), parts along dimension 0, may hold values from -40 to 40
- out_weight: bfloat16 [16384, 7168], P('pool', 'tp'), may hold values from -0.046875 to 0.046875
- norm_gain: bfloat16 [7168], P('tp'), may hold values from 0.5 to 1.5
- gate_weight: bfloat16 [7168, 18432], P('tp', 'pool'), may hold values from -0.0625 to 0.0625
- up_weight: bfloat16 [7168, 18432], P('tp', 'pool'), may hold values from -0.0625 to 0.0625
- down_weight: bfloat16 [18432, 7168], P('pool', 'tp'), may hold values from -0.046875 to 0.046875
Outputs:
- layer_out: bfloat16 [192, 7168], P(('groups', 'pool'), 'tp'), parts along dimension 0
The draws below stay inside these ranges and needn't reach their ends.
There are 2 independent parts, one for each index of `groups`. The reference program is written for one: setup_inputs(seed, part) draws one part's arguments, and reference() takes and returns one part's arrays. A program takes and returns all parts, laid end to end along the dimension named above; an argument that names none is the same for every part. Nothing has to cross between parts.
Inputs may be any that keep to these rules, and one draw needn't show every extreme that they name: `lengths`: every request has at least 2 positions in use and at most 512; some request of every draw has exactly 512.
All inputs are finite; a program needn't handle non-finite values.
Results may differ from the reference program's by a relative error of at most 0.009.
Values may be sent and summed in bfloat16 or wider, within the bound.
A program may use at most 192 MiB of HBM per device.

```python
import math
import jax
import jax.numpy as jnp
from jax import lax

D = 7168
FF = 18432
HEADS = 64
HD = 256
L = 512
REQUESTS = 96


def draw_queries(key, part):
    base = jnp.clip(jax.random.normal(jax.random.fold_in(key, 22), (REQUESTS, HEADS, HD), jnp.float32), -4.5, 4.5)
    return base.reshape(REQUESTS, HEADS * HD).astype(jnp.bfloat16)


def draw_cached_entries(key, part):
    base = jnp.clip(jax.random.normal(jax.random.fold_in(key, 24), (REQUESTS, L, 2 * HD), jnp.float32), -4.5, 4.5)
    return base.astype(jnp.bfloat16)


def draw_lengths(key, part):
    drawn = jax.random.randint(jax.random.fold_in(key, 31), (REQUESTS,), 2, L + 1)
    full_at = jax.random.randint(jax.random.fold_in(key, 32), (), 0, REQUESTS)
    return jnp.where(jnp.arange(REQUESTS) == full_at, L, drawn).astype(jnp.int32)


def draw_residual(key, part):
    row_scale = 10.0 ** jax.random.uniform(jax.random.fold_in(key, 41), (REQUESTS, 1), jnp.float32)
    ramp = jnp.arange(D).astype(jnp.float32)[None, :] / D
    col_scale = 10.0 ** (0.5 * jax.random.uniform(jax.random.fold_in(key, 42), (1, D), jnp.float32) + 0.5 * ramp)
    base = jnp.clip(jax.random.normal(jax.random.fold_in(key, 44), (REQUESTS, D), jnp.float32), -4.0, 4.0)
    return (0.1 * base * row_scale * col_scale).astype(jnp.bfloat16)


def steps_of(stream_key, extent, shards, low, high):
    level = 1.0
    for position, parts in shards:
        heights = jax.random.uniform(jax.random.fold_in(jax.random.fold_in(stream_key, 6), position), (parts,), jnp.float32, low / len(shards), high / len(shards))
        level = level * jnp.repeat(jnp.exp(heights), extent[position] // parts).reshape((-1,) + (1,) * (len(extent) - 1 - position))
    return level


def bell_draw(rng, dims, spread, bound, pieces=(), kind=jnp.bfloat16):
    values = spread * jax.random.normal(rng, dims, jnp.float32)
    if pieces:
        values = values * steps_of(rng, dims, pieces, -0.22, 0.18)
    return jnp.clip(values, -bound, bound).astype(kind)


def setup_inputs(seed: int = 0, part: int = 0) -> dict:
    key_of = jax.random.split(jax.random.key(seed), 11)
    part_keys = jax.random.split(jax.random.fold_in(key_of[10], part), 11)
    queries = draw_queries(jax.random.fold_in(jax.random.fold_in(key_of[10], part), 71), part)
    cached_entries = draw_cached_entries(jax.random.fold_in(jax.random.fold_in(key_of[10], part), 71), part)
    new_entry = bell_draw(part_keys[2], (REQUESTS, 2 * HD), 1.0, 4.5, ((0, 16),))
    lengths = draw_lengths(jax.random.fold_in(jax.random.fold_in(key_of[10], part), 71), part)
    residual = draw_residual(jax.random.fold_in(jax.random.fold_in(key_of[10], part), 71), part)
    out_weight = bell_draw(key_of[5], (HEADS * HD, D), (HEADS * HD) ** -0.5, 0.046875, ((0, 4), (1, 4)))
    norm_gain = jnp.clip(1.0 + 0.1 * jax.random.normal(key_of[6], (D,), jnp.float32), 0.5, 1.5).astype(jnp.bfloat16)
    gate_weight = bell_draw(key_of[7], (D, FF), D ** -0.5, 0.0625, ((0, 4), (1, 4)))
    up_weight = bell_draw(key_of[8], (D, FF), D ** -0.5, 0.0625, ((0, 4), (1, 4)))
    down_weight = bell_draw(key_of[9], (FF, D), FF ** -0.5, 0.046875, ((0, 4), (1, 4)))
    return {"queries": queries, "cached_entries": cached_entries, "new_entry": new_entry, "lengths": lengths, "residual": residual, "out_weight": out_weight, "norm_gain": norm_gain, "gate_weight": gate_weight, "up_weight": up_weight, "down_weight": down_weight}


def attend_one(query_row, entry_rows, new_row, length):
    query_heads = query_row.astype(jnp.float32).reshape(HEADS, HD)
    key_rows = entry_rows[:, :HD].astype(jnp.float32)
    value_rows = entry_rows[:, HD:].astype(jnp.float32)
    factor = 1.0 / math.sqrt(HD)
    scores = jnp.dot(query_heads, key_rows.T) * factor
    own_score = jnp.dot(query_heads, new_row[:HD].astype(jnp.float32)) * factor
    usable = jnp.arange(L) < length
    scores = jnp.where(usable[None, :], scores, -jnp.inf)
    peak_score = jnp.maximum(lax.optimization_barrier(jnp.max(scores, axis=1)), own_score)
    weights_raw = jnp.where(usable[None, :], jnp.exp(scores - peak_score[:, None]), 0.0)
    own_raw = jnp.exp(own_score - peak_score)
    totals = lax.optimization_barrier(jnp.sum(weights_raw, axis=1)) + own_raw
    weights = lax.optimization_barrier((weights_raw / totals[:, None]).astype(jnp.bfloat16)).astype(jnp.float32)
    own_weight = lax.optimization_barrier((own_raw / totals).astype(jnp.bfloat16)).astype(jnp.float32)
    mixture = jnp.dot(weights, value_rows) + own_weight[:, None] * new_row[HD:].astype(jnp.float32)[None, :]
    return mixture.reshape(HEADS * HD).astype(jnp.bfloat16)

def reference(queries, cached_entries, new_entry, lengths, residual, out_weight, norm_gain, gate_weight, up_weight, down_weight):
    attended = lax.map(lambda items: attend_one(items[0], items[1], items[2], items[3]), (queries, cached_entries, new_entry, lengths))
    post_attn = jnp.dot(attended, out_weight, preferred_element_type=jnp.float32) + residual.astype(jnp.float32)
    scaled = (post_attn * norm_gain.astype(jnp.float32)[None, :]).astype(jnp.bfloat16)
    inv_rms = lax.rsqrt(lax.optimization_barrier(jnp.mean(post_attn * post_attn, axis=1)) + 1e-06)
    gate_pre = jnp.dot(scaled, gate_weight, preferred_element_type=jnp.float32) * inv_rms[:, None]
    up_pre = jnp.dot(scaled, up_weight, preferred_element_type=jnp.float32) * inv_rms[:, None]
    hidden = (jax.nn.silu(gate_pre) * up_pre).astype(jnp.bfloat16)
    return (post_attn + jnp.dot(hidden, down_weight, preferred_element_type=jnp.float32)).astype(jnp.bfloat16)
```

```python
import functools
import math

import jax
import jax.numpy as jnp
import numpy as np
from jax import lax
from jax.experimental import pallas as pl
from jax.experimental.pallas import tpu as pltpu
from jax.sharding import PartitionSpec as P

D = 7168
HEADS = 64
HD = 256


epsilon = 1e-06


def attend(queries, cached_entries, new_entry, lengths):
    amount = queries.shape[0]
    query_heads = queries.reshape(amount, HEADS, HD)
    key_rows = cached_entries[:, :, :HD]
    value_rows = cached_entries[:, :, HD:]
    factor = 1.0 / math.sqrt(HD)
    scores = (
        jnp.einsum("rhd,rld->rhl", query_heads, key_rows, preferred_element_type=jnp.float32)
        * factor
    )
    own_score = (
        jnp.einsum("rhd,rd->rh", query_heads, new_entry[:, :HD], preferred_element_type=jnp.float32)
        * factor
    )
    positions = lax.broadcasted_iota(jnp.int32, scores.shape, 2)
    usable = positions < lengths[:, None, None]
    scores = jnp.where(usable, scores, -jnp.inf)
    peak_score = jnp.maximum(jnp.max(scores, axis=2), own_score)
    weights_raw = jnp.where(usable, jnp.exp(scores - peak_score[:, :, None]), 0.0)
    own_raw = jnp.exp(own_score - peak_score)
    totals = jnp.sum(weights_raw, axis=2) + own_raw
    weights = (weights_raw / totals[:, :, None]).astype(jnp.bfloat16)
    own_weight = (own_raw / totals).astype(jnp.bfloat16)
    mixture = jnp.einsum("rhl,rld->rhd", weights, value_rows, preferred_element_type=jnp.float32)
    mixture = mixture + own_weight.astype(jnp.float32)[:, :, None] * new_entry[:, None, HD:].astype(
        jnp.float32
    )
    return mixture.reshape(amount, HEADS * HD).astype(jnp.bfloat16)


PAD = 8
LAG = 2
SLOTS = 8
MESH = pl.DeviceIdType.MESH


def tile_of(extent):
    return 256 if extent % 256 == 0 else 128


def layer_kernel(
    pools,
    tps,
    att,
    resid,
    gain,
    pick_local,
    pick_all,
    wo_hbm,
    wg_hbm,
    wu_hbm,
    wd_hbm,
    out,
    wo,
    wg,
    wu,
    wd,
    raw,
    stage,
    slabs,
    x,
    pf,
    psend,
    precv,
    drecv,
    own_post,
    scl,
    sq_all,
    sq,
    sq_recv,
    s_in,
    part,
    sbuf,
    rbuf,
    hid,
    acc,
    w_sem,
    g_sem,
    u_sem,
    a_send,
    a_recv,
    c_right,
    c_left,
    c_recv,
    p_send,
    p_recv,
    s_send,
    s_recv,
    q_send,
    q_recv,
    e_send,
    e_recv,
    r_send,
    r_recv,
    h_send,
    h_recv,
    d_send,
    d_recv,
):
    p = lax.axis_index("pool")
    t = lax.axis_index("tp")
    block = resid.shape[0]
    width = resid.shape[1]
    pad, cols = att.shape[1], att.shape[2]
    slab_rows = slabs.shape[1]
    rows = x.shape[0]
    tile = part.shape[3]
    tiles = part.shape[0]
    pairs = (tiles + 1) // 2
    slots = wg.shape[0]
    out_tile = tile_of(width)
    last = tps - 1
    before, behind = lax.rem(t + tps - 1, tps), lax.rem(t + 1, tps)

    def weight_copies(j):
        slot = lax.rem(j, slots)
        at = pl.ds(pl.multiple_of(j * tile, tile), tile)
        return (
            pltpu.make_async_copy(wg_hbm.at[:, at], wg.at[slot], g_sem.at[slot]),
            pltpu.make_async_copy(wu_hbm.at[:, at], wu.at[slot], u_sem.at[slot]),
        )

    wo_copy = pltpu.make_async_copy(wo_hbm, wo, w_sem.at[0])
    wd_copy = pltpu.make_async_copy(wd_hbm, wd, w_sem.at[1])
    wo_copy.start()

    barrier = pltpu.get_barrier_semaphore()
    for k in range(1, pools):
        pl.semaphore_signal(
            barrier, inc=1, device_id={"pool": lax.rem(p + k, pools)}, device_id_type=MESH
        )

    @pl.when(t > 0)
    def _():
        pl.semaphore_signal(barrier, inc=1, device_id={"tp": before}, device_id_type=MESH)

    @pl.when(t < last)
    def _():
        pl.semaphore_signal(barrier, inc=1, device_id={"tp": behind}, device_id_type=MESH)

    peers = pools - 1 + lax.convert_element_type(t > 0, jnp.int32)
    pl.semaphore_wait(barrier, peers + lax.convert_element_type(t < last, jnp.int32))

    def remote(src, dst, send, recv, device):
        return pltpu.make_async_remote_copy(
            src_ref=src,
            dst_ref=dst,
            send_sem=send,
            recv_sem=recv,
            device_id=device,
            device_id_type=MESH,
        )

    def pool_peer(k):
        return lax.rem(p + k, pools)

    def att_copy(k):
        q = pool_peer(k)
        return remote(att.at[q], raw.at[p], a_send.at[k], a_recv.at[p], {"pool": q})

    def att_arrival(k):
        q = pool_peer(k)
        return remote(att.at[q], raw.at[q], a_send.at[k], a_recv.at[q], {"pool": q})

    for k in range(1, pools):
        att_copy(k).start()

    for j in range(min(slots, tiles)):
        for copy in weight_copies(jnp.int32(j)):
            copy.start()
    wd_copy.start()

    stage[pl.ds(pl.multiple_of(p * pad, 8), pad), :] = att[p].astype(jnp.float32)
    for k in range(1, pools):
        att_arrival(k).wait_recv()
        q = pool_peer(k)
        stage[pl.ds(pl.multiple_of(q * pad, 8), pad), :] = raw[q].astype(jnp.float32)
    slabs[t] = jnp.dot(
        pick_local[...],
        stage[pl.ds(0, pools * pad), :].astype(jnp.bfloat16),
        preferred_element_type=jnp.float32,
    ).astype(jnp.bfloat16)

    def slab_right(origin):
        return remote(
            slabs.at[origin], slabs.at[origin], c_right.at[origin], c_recv.at[origin], {"tp": behind}
        )

    def slab_left(origin):
        return remote(
            slabs.at[origin], slabs.at[origin], c_left.at[origin], c_recv.at[origin], {"tp": before}
        )

    @pl.when(t < last)
    def _():
        slab_right(t).start()

    @pl.when(t > 0)
    def _():
        slab_left(t).start()

    for k in range(1, tps):

        @pl.when(t - k >= 0)
        def _():
            slab_left(t - k).wait_recv()

            @pl.when(t < last)
            def _():
                slab_right(t - k).start()

        @pl.when(t + k <= last)
        def _():
            slab_right(t + k).wait_recv()

            @pl.when(t > 0)
            def _():
                slab_left(t + k).start()

    for origin in range(tps):
        stage[pl.ds(origin * slab_rows, slab_rows), :] = slabs[origin].astype(jnp.float32)
    step_cols = tile_of(cols)

    @pl.loop(0, cols // step_cols)
    def _(n):
        at = pl.ds(pl.multiple_of(n * step_cols, step_cols), step_cols)
        x[:, at] = jnp.dot(
            pick_all[...],
            stage[pl.ds(0, rows), at].astype(jnp.bfloat16),
            preferred_element_type=jnp.float32,
        ).astype(jnp.bfloat16)

    wo_copy.wait()

    @pl.loop(0, width // out_tile)
    def _(n):
        at = pl.ds(pl.multiple_of(n * out_tile, out_tile), out_tile)
        value = jnp.dot(x[...], wo[:, at], preferred_element_type=jnp.float32)
        pf[:, at] = value
        for q in range(pools):
            psend[q, :, at] = value[q * block : (q + 1) * block].astype(jnp.bfloat16)

    def part_copy(k):
        q = pool_peer(k)
        return remote(psend.at[q], precv.at[p], p_send.at[k], p_recv.at[p], {"pool": q})

    def part_arrival(k):
        q = pool_peer(k)
        return remote(psend.at[q], precv.at[q], p_send.at[k], p_recv.at[q], {"pool": q})

    for k in range(1, pools):
        part_copy(k).start()
    post = pf[pl.ds(pl.multiple_of(p * block, 8), block), :] + resid[...].astype(jnp.float32)
    for k in range(1, pools):
        part_arrival(k).wait_recv()
        post = post + precv[pool_peer(k)].astype(jnp.float32)
    own_post[...] = post
    scl[p] = (post * gain[...]).astype(jnp.bfloat16)
    sq_all[p] = jnp.broadcast_to(jnp.sum(post * post, axis=1, keepdims=True), (block, 128))

    def scaled_copy(k):
        q = pool_peer(k)
        return remote(scl.at[p], scl.at[p], s_send.at[k], s_recv.at[p], {"pool": q})

    def scaled_arrival(k):
        q = pool_peer(k)
        return remote(scl.at[q], scl.at[q], s_send.at[k], s_recv.at[q], {"pool": q})

    def square_copy(k):
        q = pool_peer(k)
        return remote(sq_all.at[p], sq_all.at[p], q_send.at[k], q_recv.at[p], {"pool": q})

    def square_arrival(k):
        q = pool_peer(k)
        return remote(sq_all.at[q], sq_all.at[q], q_send.at[k], q_recv.at[q], {"pool": q})

    for k in range(1, pools):
        square_copy(k).start()
        scaled_copy(k).start()
    for k in range(1, pools):
        square_arrival(k).wait_recv()
        scaled_arrival(k).wait_recv()
    for q in range(pools):
        pf[pl.ds(q * block, block), :] = scl[q].astype(jnp.float32)
        for s in range(2):
            sq[s, pl.ds(q * block, block), :] = sq_all[q]
    s_in[...] = pf[...].astype(jnp.bfloat16)
    acc[...] = jnp.zeros_like(acc)

    def lanes(s):
        if s == 0:
            return last - t, before, behind
        return t, behind, before

    def square_hop(s):
        _, after, _ = lanes(s)
        return remote(sq.at[s], sq_recv.at[s], e_send.at[s], e_recv.at[s], {"tp": after})

    def sum_hop(s, j):
        _, after, _ = lanes(s)
        return remote(sbuf.at[j], rbuf.at[j], r_send.at[j], r_recv.at[j], {"tp": after})

    def hidden_hop(s, j):
        _, _, back = lanes(s)
        return remote(hid.at[j], hid.at[j], h_send.at[j], h_recv.at[j], {"tp": back})

    def down(j):
        piece = hid[j]
        at = pl.ds(pl.multiple_of(j * tile, tile), tile)

        @pl.loop(0, width // out_tile)
        def _(n):
            here = pl.ds(pl.multiple_of(n * out_tile, out_tile), out_tile)
            acc[:, here] += jnp.dot(piece, wd[at, here], preferred_element_type=jnp.float32)

    wd_copy.wait()

    def one_step(i):
        for s in range(2):
            j = 2 * i + s

            @pl.when(j < tiles)
            def _():
                slot = lax.rem(j, slots)
                for copy in weight_copies(j):
                    copy.wait()
                part[j, 0] = jnp.dot(s_in[...], wg[slot], preferred_element_type=jnp.float32)
                part[j, 1] = jnp.dot(s_in[...], wu[slot], preferred_element_type=jnp.float32)

                @pl.when(j + slots < tiles)
                def _():
                    for copy in weight_copies(j + slots):
                        copy.start()

        for s in range(2):
            far, _, _ = lanes(s)
            c = i - LAG * far
            j = 2 * c + s

            @pl.when((c >= 0) & (j < tiles))
            def _():
                @pl.when(far > 0)
                def _():
                    @pl.when(c == 0)
                    def _():
                        square_hop(s).wait_recv()
                        sq[s] = sq[s] + sq_recv[s]

                    sum_hop(s, j).wait_recv()
                    part[j] = part[j] + rbuf[j].astype(jnp.float32)

                @pl.when(far < last)
                def _():
                    @pl.when(c == 0)
                    def _():
                        square_hop(s).start()

                    sbuf[j] = part[j].astype(jnp.bfloat16)
                    sum_hop(s, j).start()

                @pl.when(far == last)
                def _():
                    inv = lax.rsqrt(sq[s][:, :1] / D + epsilon)
                    gate = part[j, 0] * inv
                    up = part[j, 1] * inv
                    hid[j] = (gate / (1.0 + jnp.exp(-gate)) * up).astype(jnp.bfloat16)
                    if tps > 1:
                        hidden_hop(s, j).start()
                    down(j)

        for s in range(2):
            far, _, _ = lanes(s)
            back = last - far
            c = i - LAG * last - LAG * back
            j = 2 * c + s

            @pl.when((back > 0) & (c >= 0) & (j < tiles))
            def _():
                hidden_hop(s, j).wait_recv()

                @pl.when(back < last)
                def _():
                    hidden_hop(s, j).start()

                down(j)

    pl.loop(0, pairs + 2 * LAG * last)(one_step)

    for k in range(1, pools):
        part_copy(k).wait_send()

    @pl.loop(0, width // out_tile)
    def _(n):
        at = pl.ds(pl.multiple_of(n * out_tile, out_tile), out_tile)
        value = acc[:, at]
        for q in range(pools):
            psend[q, :, at] = value[q * block : (q + 1) * block].astype(jnp.bfloat16)

    def down_copy(k):
        q = pool_peer(k)
        return remote(psend.at[q], drecv.at[p], d_send.at[k], d_recv.at[p], {"pool": q})

    def down_arrival(k):
        q = pool_peer(k)
        return remote(psend.at[q], drecv.at[q], d_send.at[k], d_recv.at[q], {"pool": q})

    for k in range(1, pools):
        down_copy(k).start()
    total = own_post[...] + acc[pl.ds(pl.multiple_of(p * block, 8), block), :]
    for k in range(1, pools):
        down_arrival(k).wait_recv()
        total = total + drecv[pool_peer(k)].astype(jnp.float32)
    out[...] = total.astype(jnp.bfloat16)

    for k in range(1, pools):
        att_copy(k).wait_send()
        scaled_copy(k).wait_send()
        square_copy(k).wait_send()
        down_copy(k).wait_send()
    for origin in range(tps):

        @pl.when((t < last) & (origin <= t))
        def _():
            slab_right(origin).wait_send()

        @pl.when((t > 0) & (origin >= t))
        def _():
            slab_left(origin).wait_send()

    for s in range(2):
        far, _, _ = lanes(s)

        @pl.when(far < last)
        def _():
            square_hop(s).wait_send()

    @pl.loop(0, pairs)
    def _(c):
        for s in range(2):
            far, _, _ = lanes(s)
            j = 2 * c + s

            @pl.when((far < last) & (j < tiles))
            def _():
                sum_hop(s, j).wait_send()

            @pl.when((far > 0) & (j < tiles))
            def _():
                hidden_hop(s, j).wait_send()


def finish_rows(att, resid, gain, out_weight, gate_weight, up_weight, down_weight, amount):
    pools, tps = lax.axis_size("pool"), lax.axis_size("tp")
    block, width = resid.shape
    pad, cols = att.shape[1], att.shape[2]
    ff = gate_weight.shape[1]
    slab_rows = pools * amount
    rows = slab_rows * tps
    tile = tile_of(ff)
    tiles = ff // tile
    slots = min(SLOTS, tiles)

    local = np.arange(slab_rows)
    pick_local = np.zeros((slab_rows, pools * pad), np.float32)
    pick_local[local, local // amount * pad + local % amount] = 1
    every = np.arange(rows)
    of_pool, of_tp, of_row = every // block, every // amount % tps, every % amount
    pick_all = np.zeros((rows, rows), np.float32)
    pick_all[every, (of_tp * pools + of_pool) * amount + of_row] = 1

    vmem = pl.BlockSpec(memory_space=pltpu.VMEM)
    anywhere = pl.BlockSpec(memory_space=pl.ANY)
    bf16, f32 = jnp.bfloat16, jnp.float32
    dma = pltpu.SemaphoreType.DMA
    scratch = [
        pltpu.VMEM(out_weight.shape, bf16),
        pltpu.VMEM((slots, gate_weight.shape[0], tile), bf16),
        pltpu.VMEM((slots, gate_weight.shape[0], tile), bf16),
        pltpu.VMEM(down_weight.shape, bf16),
        pltpu.VMEM((pools, pad, cols), bf16),
        pltpu.VMEM((max(rows, pools * pad), cols), f32),
        pltpu.VMEM((tps, slab_rows, cols), bf16),
        pltpu.VMEM((rows, cols), bf16),
        pltpu.VMEM((rows, width), f32),
        pltpu.VMEM((pools, block, width), bf16),
        pltpu.VMEM((pools, block, width), bf16),
        pltpu.VMEM((pools, block, width), bf16),
        pltpu.VMEM((block, width), f32),
        pltpu.VMEM((pools, block, width), bf16),
        pltpu.VMEM((pools, block, 128), f32),
        pltpu.VMEM((2, rows, 128), f32),
        pltpu.VMEM((2, rows, 128), f32),
        pltpu.VMEM((rows, width), bf16),
        pltpu.VMEM((tiles, 2, rows, tile), f32),
        pltpu.VMEM((tiles, 2, rows, tile), bf16),
        pltpu.VMEM((tiles, 2, rows, tile), bf16),
        pltpu.VMEM((tiles, rows, tile), bf16),
        pltpu.VMEM((rows, width), f32),
        dma((2,)),
        dma((slots,)),
        dma((slots,)),
        dma((pools,)),
        dma((pools,)),
        dma((tps,)),
        dma((tps,)),
        dma((tps,)),
        dma((pools,)),
        dma((pools,)),
        dma((pools,)),
        dma((pools,)),
        dma((pools,)),
        dma((pools,)),
        dma((2,)),
        dma((2,)),
        dma((tiles,)),
        dma((tiles,)),
        dma((tiles,)),
        dma((tiles,)),
        dma((pools,)),
        dma((pools,)),
    ]
    return pl.pallas_call(
        functools.partial(layer_kernel, pools, tps),
        out_shape=jax.ShapeDtypeStruct((block, width), bf16),
        in_specs=[vmem] * 5 + [anywhere] * 4,
        out_specs=vmem,
        scratch_shapes=scratch,
        compiler_params=pltpu.CompilerParams(
            collective_id=0, has_side_effects=True, vmem_limit_bytes=62 << 20
        ),
        name="layer",
    )(
        att,
        resid,
        gain,
        jnp.asarray(pick_local, bf16),
        jnp.asarray(pick_all, bf16),
        out_weight,
        gate_weight,
        up_weight,
        down_weight,
    )


def on_device(
    queries,
    cached_entries,
    new_entry,
    lengths,
    residual,
    out_weight,
    norm_gain,
    gate_weight,
    up_weight,
    down_weight,
):
    pools = lax.axis_size("pool")
    amount = queries.shape[0]
    pad = -(-amount // PAD) * PAD
    attended = attend(queries, cached_entries, new_entry, lengths)
    att = attended.reshape(amount, pools, -1).transpose(1, 0, 2)
    att = jnp.pad(att, ((0, 0), (0, pad - amount), (0, 0)))
    return finish_rows(
        att,
        residual,
        norm_gain.astype(jnp.float32)[None, :],
        out_weight,
        gate_weight,
        up_weight,
        down_weight,
        amount,
    )


def solution(mesh):
    placed = (
        P(("groups", "pool", "tp"), None),
        P(("groups", "pool", "tp"), None, None),
        P(("groups", "pool", "tp"), None),
        P(("groups", "pool", "tp")),
        P(("groups", "pool"), "tp"),
        P("pool", "tp"),
        P("tp"),
        P("tp", "pool"),
        P("tp", "pool"),
        P("pool", "tp"),
    )
    return jax.shard_map(
        on_device,
        mesh=mesh,
        in_specs=placed,
        out_specs=P(("groups", "pool"), "tp"),
        check_vma=False,
    )
```

```python
import functools
import math

import jax
import jax.numpy as jnp
import numpy as np
from jax import lax
from jax.experimental import pallas as pl
from jax.experimental.pallas import tpu as pltpu
from jax.sharding import PartitionSpec as P

D = 7168
HEADS = 64
HD = 256


epsilon = 1e-06


def attend(queries, cached_entries, new_entry, lengths):
    amount = queries.shape[0]
    query_heads = queries.reshape(amount, HEADS, HD)
    key_rows = cached_entries[:, :, :HD]
    value_rows = cached_entries[:, :, HD:]
    factor = 1.0 / math.sqrt(HD)
    scores = (
        jnp.einsum("rhd,rld->rhl", query_heads, key_rows, preferred_element_type=jnp.float32)
        * factor
    )
    own_score = (
        jnp.einsum("rhd,rd->rh", query_heads, new_entry[:, :HD], preferred_element_type=jnp.float32)
        * factor
    )
    positions = lax.broadcasted_iota(jnp.int32, scores.shape, 2)
    usable = positions < lengths[:, None, None]
    scores = jnp.where(usable, scores, -jnp.inf)
    peak_score = jnp.maximum(jnp.max(scores, axis=2), own_score)
    weights_raw = jnp.where(usable, jnp.exp(scores - peak_score[:, :, None]), 0.0)
    own_raw = jnp.exp(own_score - peak_score)
    totals = jnp.sum(weights_raw, axis=2) + own_raw
    weights = (weights_raw / totals[:, :, None]).astype(jnp.bfloat16)
    own_weight = (own_raw / totals).astype(jnp.bfloat16)
    mixture = jnp.einsum("rhl,rld->rhd", weights, value_rows, preferred_element_type=jnp.float32)
    mixture = mixture + own_weight.astype(jnp.float32)[:, :, None] * new_entry[:, None, HD:].astype(
        jnp.float32
    )
    return mixture.reshape(amount, HEADS * HD).astype(jnp.bfloat16)


PAD = 8
LAG = 2
SLOTS = 8
MESH = pl.DeviceIdType.MESH


def tile_of(extent):
    return 256 if extent % 256 == 0 else 128


def layer_kernel(
    pools,
    tps,
    att,
    resid,
    gain,
    pick_local,
    pick_all,
    wo_hbm,
    wg_hbm,
    wu_hbm,
    wd_hbm,
    out,
    wo,
    wg,
    wu,
    wd,
    raw,
    stage,
    slabs,
    x,
    pf,
    psend,
    precv,
    drecv,
    own_post,
    scl,
    sq_all,
    sq,
    sq_recv,
    s_in,
    part,
    sbuf,
    rbuf,
    hid,
    acc,
    w_sem,
    g_sem,
    u_sem,
    a_send,
    a_recv,
    c_right,
    c_left,
    c_recv,
    p_send,
    p_recv,
    s_send,
    s_recv,
    q_send,
    q_recv,
    e_send,
    e_recv,
    r_send,
    r_recv,
    h_send,
    h_recv,
    d_send,
    d_recv,
):
    p = lax.axis_index("pool")
    t = lax.axis_index("tp")
    block = resid.shape[0]
    width = resid.shape[1]
    pad, cols = att.shape[1], att.shape[2]
    slab_rows = slabs.shape[1]
    rows = x.shape[0]
    tile = part.shape[3]
    tiles = part.shape[0]
    pairs = (tiles + 1) // 2
    slots = wg.shape[0]
    out_tile = tile_of(width)
    last = tps - 1
    before, behind = lax.rem(t + tps - 1, tps), lax.rem(t + 1, tps)

    def weight_copies(j):
        slot = lax.rem(j, slots)
        at = pl.ds(pl.multiple_of(j * tile, tile), tile)
        return (
            pltpu.make_async_copy(wg_hbm.at[:, at], wg.at[slot], g_sem.at[slot]),
            pltpu.make_async_copy(wu_hbm.at[:, at], wu.at[slot], u_sem.at[slot]),
        )

    wo_copy = pltpu.make_async_copy(wo_hbm, wo, w_sem.at[0])
    wd_copy = pltpu.make_async_copy(wd_hbm, wd, w_sem.at[1])
    wo_copy.start()

    barrier = pltpu.get_barrier_semaphore()
    for k in range(1, pools):
        pl.semaphore_signal(
            barrier, inc=1, device_id={"pool": lax.rem(p + k, pools)}, device_id_type=MESH
        )

    @pl.when(t > 0)
    def _():
        pl.semaphore_signal(barrier, inc=1, device_id={"tp": before}, device_id_type=MESH)

    @pl.when(t < last)
    def _():
        pl.semaphore_signal(barrier, inc=1, device_id={"tp": behind}, device_id_type=MESH)

    peers = pools - 1 + lax.convert_element_type(t > 0, jnp.int32)
    pl.semaphore_wait(barrier, peers + lax.convert_element_type(t < last, jnp.int32))

    def remote(src, dst, send, recv, device):
        return pltpu.make_async_remote_copy(
            src_ref=src,
            dst_ref=dst,
            send_sem=send,
            recv_sem=recv,
            device_id=device,
            device_id_type=MESH,
        )

    def pool_peer(k):
        return lax.rem(p + k, pools)

    def att_copy(k):
        q = pool_peer(k)
        return remote(att.at[q], raw.at[p], a_send.at[k], a_recv.at[p], {"pool": q})

    def att_arrival(k):
        q = pool_peer(k)
        return remote(att.at[q], raw.at[q], a_send.at[k], a_recv.at[q], {"pool": q})

    for k in range(1, pools):
        att_copy(k).start()

    for j in range(min(slots, tiles)):
        for copy in weight_copies(jnp.int32(j)):
            copy.start()
    wd_copy.start()

    stage[pl.ds(pl.multiple_of(p * pad, 8), pad), :] = att[p].astype(jnp.float32)
    for k in range(1, pools):
        att_arrival(k).wait_recv()
        q = pool_peer(k)
        stage[pl.ds(pl.multiple_of(q * pad, 8), pad), :] = raw[q].astype(jnp.float32)
    slabs[t] = jnp.dot(
        pick_local[...],
        stage[pl.ds(0, pools * pad), :].astype(jnp.bfloat16),
        preferred_element_type=jnp.float32,
    ).astype(jnp.bfloat16)

    def slab_right(origin):
        return remote(
            slabs.at[origin], slabs.at[origin], c_right.at[origin], c_recv.at[origin], {"tp": behind}
        )

    def slab_left(origin):
        return remote(
            slabs.at[origin], slabs.at[origin], c_left.at[origin], c_recv.at[origin], {"tp": before}
        )

    @pl.when(t < last)
    def _():
        slab_right(t).start()

    @pl.when(t > 0)
    def _():
        slab_left(t).start()

    for k in range(1, tps):

        @pl.when(t - k >= 0)
        def _():
            slab_left(t - k).wait_recv()

            @pl.when(t < last)
            def _():
                slab_right(t - k).start()

        @pl.when(t + k <= last)
        def _():
            slab_right(t + k).wait_recv()

            @pl.when(t > 0)
            def _():
                slab_left(t + k).start()

    for origin in range(tps):
        stage[pl.ds(origin * slab_rows, slab_rows), :] = slabs[origin].astype(jnp.float32)
    step_cols = tile_of(cols)

    @pl.loop(0, cols // step_cols)
    def _(n):
        at = pl.ds(pl.multiple_of(n * step_cols, step_cols), step_cols)
        x[:, at] = jnp.dot(
            pick_all[...],
            stage[pl.ds(0, rows), at].astype(jnp.bfloat16),
            preferred_element_type=jnp.float32,
        ).astype(jnp.bfloat16)

    wo_copy.wait()

    @pl.loop(0, width // out_tile)
    def _(n):
        at = pl.ds(pl.multiple_of(n * out_tile, out_tile), out_tile)
        value = jnp.dot(x[...], wo[:, at], preferred_element_type=jnp.float32)
        pf[:, at] = value
        for q in range(pools):
            psend[q, :, at] = value[q * block : (q + 1) * block].astype(jnp.bfloat16)

    def part_copy(k):
        q = pool_peer(k)
        return remote(psend.at[q], precv.at[p], p_send.at[k], p_recv.at[p], {"pool": q})

    def part_arrival(k):
        q = pool_peer(k)
        return remote(psend.at[q], precv.at[q], p_send.at[k], p_recv.at[q], {"pool": q})

    for k in range(1, pools):
        part_copy(k).start()
    post = pf[pl.ds(pl.multiple_of(p * block, 8), block), :] + resid[...].astype(jnp.float32)
    for k in range(1, pools):
        part_arrival(k).wait_recv()
        post = post + precv[pool_peer(k)].astype(jnp.float32)
    own_post[...] = post
    scl[p] = (post * gain[...]).astype(jnp.bfloat16)
    sq_all[p] = jnp.broadcast_to(jnp.sum(post * post, axis=1, keepdims=True), (block, 128))

    def scaled_copy(k):
        q = pool_peer(k)
        return remote(scl.at[p], scl.at[p], s_send.at[k], s_recv.at[p], {"pool": q})

    def scaled_arrival(k):
        q = pool_peer(k)
        return remote(scl.at[q], scl.at[q], s_send.at[k], s_recv.at[q], {"pool": q})

    def square_copy(k):
        q = pool_peer(k)
        return remote(sq_all.at[p], sq_all.at[p], q_send.at[k], q_recv.at[p], {"pool": q})

    def square_arrival(k):
        q = pool_peer(k)
        return remote(sq_all.at[q], sq_all.at[q], q_send.at[k], q_recv.at[q], {"pool": q})

    for k in range(1, pools):
        square_copy(k).start()
        scaled_copy(k).start()
    for k in range(1, pools):
        square_arrival(k).wait_recv()
        scaled_arrival(k).wait_recv()
    for q in range(pools):
        pf[pl.ds(q * block, block), :] = scl[q].astype(jnp.float32)
        for s in range(2):
            sq[s, pl.ds(q * block, block), :] = sq_all[q]
    s_in[...] = pf[...].astype(jnp.bfloat16)
    acc[...] = jnp.zeros_like(acc)

    def lanes(s):
        if s == 0:
            return last - t, before, behind
        return t, behind, before

    def square_hop(s):
        _, after, _ = lanes(s)
        return remote(sq.at[s], sq_recv.at[s], e_send.at[s], e_recv.at[s], {"tp": after})

    def sum_hop(s, j):
        _, after, _ = lanes(s)
        return remote(sbuf.at[j], rbuf.at[j], r_send.at[j], r_recv.at[j], {"tp": after})

    def hidden_hop(s, j):
        _, _, back = lanes(s)
        return remote(hid.at[j], hid.at[j], h_send.at[j], h_recv.at[j], {"tp": back})

    def down(j):
        piece = hid[j]
        at = pl.ds(pl.multiple_of(j * tile, tile), tile)

        @pl.loop(0, width // out_tile)
        def _(n):
            here = pl.ds(pl.multiple_of(n * out_tile, out_tile), out_tile)
            acc[:, here] += jnp.dot(piece, wd[at, here], preferred_element_type=jnp.float32)

    wd_copy.wait()

    def one_step(i):
        for s in range(2):
            j = 2 * i + s

            @pl.when(j < tiles)
            def _():
                slot = lax.rem(j, slots)
                for copy in weight_copies(j):
                    copy.wait()
                part[j, 0] = jnp.dot(s_in[...], wg[slot], preferred_element_type=jnp.float32)
                part[j, 1] = jnp.dot(s_in[...], wu[slot], preferred_element_type=jnp.float32)

                @pl.when(j + slots < tiles)
                def _():
                    for copy in weight_copies(j + slots):
                        copy.start()

            far, _, _ = lanes(s)
            c = i - LAG * far
            j = 2 * c + s

            @pl.when((c >= 0) & (j < tiles))
            def _():
                @pl.when(far > 0)
                def _():
                    @pl.when(c == 0)
                    def _():
                        square_hop(s).wait_recv()
                        sq[s] = sq[s] + sq_recv[s]

                    sum_hop(s, j).wait_recv()
                    part[j] = part[j] + rbuf[j].astype(jnp.float32)

                @pl.when(far < last)
                def _():
                    @pl.when(c == 0)
                    def _():
                        square_hop(s).start()

                    sbuf[j] = part[j].astype(jnp.bfloat16)
                    sum_hop(s, j).start()

                @pl.when(far == last)
                def _():
                    inv = lax.rsqrt(sq[s][:, :1] / D + epsilon)
                    gate = part[j, 0] * inv
                    up = part[j, 1] * inv
                    hid[j] = (gate / (1.0 + jnp.exp(-gate)) * up).astype(jnp.bfloat16)
                    if tps > 1:
                        hidden_hop(s, j).start()
                    down(j)

        for s in range(2):
            far, _, _ = lanes(s)
            back = last - far
            c = i - LAG * last - LAG * back
            j = 2 * c + s

            @pl.when((back > 0) & (c >= 0) & (j < tiles))
            def _():
                hidden_hop(s, j).wait_recv()

                @pl.when(back < last)
                def _():
                    hidden_hop(s, j).start()

                down(j)

    pl.loop(0, pairs + 2 * LAG * last)(one_step)

    for k in range(1, pools):
        part_copy(k).wait_send()

    @pl.loop(0, width // out_tile)
    def _(n):
        at = pl.ds(pl.multiple_of(n * out_tile, out_tile), out_tile)
        value = acc[:, at]
        for q in range(pools):
            psend[q, :, at] = value[q * block : (q + 1) * block].astype(jnp.bfloat16)

    def down_copy(k):
        q = pool_peer(k)
        return remote(psend.at[q], drecv.at[p], d_send.at[k], d_recv.at[p], {"pool": q})

    def down_arrival(k):
        q = pool_peer(k)
        return remote(psend.at[q], drecv.at[q], d_send.at[k], d_recv.at[q], {"pool": q})

    for k in range(1, pools):
        down_copy(k).start()
    total = own_post[...] + acc[pl.ds(pl.multiple_of(p * block, 8), block), :]
    for k in range(1, pools):
        down_arrival(k).wait_recv()
        total = total + drecv[pool_peer(k)].astype(jnp.float32)
    out[...] = total.astype(jnp.bfloat16)

    for k in range(1, pools):
        att_copy(k).wait_send()
        scaled_copy(k).wait_send()
        square_copy(k).wait_send()
        down_copy(k).wait_send()
    for origin in range(tps):

        @pl.when((t < last) & (origin <= t))
        def _():
            slab_right(origin).wait_send()

        @pl.when((t > 0) & (origin >= t))
        def _():
            slab_left(origin).wait_send()

    for s in range(2):
        far, _, _ = lanes(s)

        @pl.when(far < last)
        def _():
            square_hop(s).wait_send()

    @pl.loop(0, pairs)
    def _(c):
        for s in range(2):
            far, _, _ = lanes(s)
            j = 2 * c + s

            @pl.when((far < last) & (j < tiles))
            def _():
                sum_hop(s, j).wait_send()

            @pl.when((far > 0) & (j < tiles))
            def _():
                hidden_hop(s, j).wait_send()


def finish_rows(att, resid, gain, out_weight, gate_weight, up_weight, down_weight, amount):
    pools, tps = lax.axis_size("pool"), lax.axis_size("tp")
    block, width = resid.shape
    pad, cols = att.shape[1], att.shape[2]
    ff = gate_weight.shape[1]
    slab_rows = pools * amount
    rows = slab_rows * tps
    tile = tile_of(ff)
    tiles = ff // tile
    slots = min(SLOTS, tiles)

    local = np.arange(slab_rows)
    pick_local = np.zeros((slab_rows, pools * pad), np.float32)
    pick_local[local, local // amount * pad + local % amount] = 1
    every = np.arange(rows)
    of_pool, of_tp, of_row = every // block, every // amount % tps, every % amount
    pick_all = np.zeros((rows, rows), np.float32)
    pick_all[every, (of_tp * pools + of_pool) * amount + of_row] = 1

    vmem = pl.BlockSpec(memory_space=pltpu.VMEM)
    anywhere = pl.BlockSpec(memory_space=pl.ANY)
    bf16, f32 = jnp.bfloat16, jnp.float32
    dma = pltpu.SemaphoreType.DMA
    scratch = [
        pltpu.VMEM(out_weight.shape, bf16),
        pltpu.VMEM((slots, gate_weight.shape[0], tile), bf16),
        pltpu.VMEM((slots, gate_weight.shape[0], tile), bf16),
        pltpu.VMEM(down_weight.shape, bf16),
        pltpu.VMEM((pools, pad, cols), bf16),
        pltpu.VMEM((max(rows, pools * pad), cols), f32),
        pltpu.VMEM((tps, slab_rows, cols), bf16),
        pltpu.VMEM((rows, cols), bf16),
        pltpu.VMEM((rows, width), f32),
        pltpu.VMEM((pools, block, width), bf16),
        pltpu.VMEM((pools, block, width), bf16),
        pltpu.VMEM((pools, block, width), bf16),
        pltpu.VMEM((block, width), f32),
        pltpu.VMEM((pools, block, width), bf16),
        pltpu.VMEM((pools, block, 128), f32),
        pltpu.VMEM((2, rows, 128), f32),
        pltpu.VMEM((2, rows, 128), f32),
        pltpu.VMEM((rows, width), bf16),
        pltpu.VMEM((tiles, 2, rows, tile), f32),
        pltpu.VMEM((tiles, 2, rows, tile), bf16),
        pltpu.VMEM((tiles, 2, rows, tile), bf16),
        pltpu.VMEM((tiles, rows, tile), bf16),
        pltpu.VMEM((rows, width), f32),
        dma((2,)),
        dma((slots,)),
        dma((slots,)),
        dma((pools,)),
        dma((pools,)),
        dma((tps,)),
        dma((tps,)),
        dma((tps,)),
        dma((pools,)),
        dma((pools,)),
        dma((pools,)),
        dma((pools,)),
        dma((pools,)),
        dma((pools,)),
        dma((2,)),
        dma((2,)),
        dma((tiles,)),
        dma((tiles,)),
        dma((tiles,)),
        dma((tiles,)),
        dma((pools,)),
        dma((pools,)),
    ]
    return pl.pallas_call(
        functools.partial(layer_kernel, pools, tps),
        out_shape=jax.ShapeDtypeStruct((block, width), bf16),
        in_specs=[vmem] * 5 + [anywhere] * 4,
        out_specs=vmem,
        scratch_shapes=scratch,
        compiler_params=pltpu.CompilerParams(
            collective_id=0, has_side_effects=True, vmem_limit_bytes=62 << 20
        ),
        name="layer",
    )(
        att,
        resid,
        gain,
        jnp.asarray(pick_local, bf16),
        jnp.asarray(pick_all, bf16),
        out_weight,
        gate_weight,
        up_weight,
        down_weight,
    )


def on_device(
    queries,
    cached_entries,
    new_entry,
    lengths,
    residual,
    out_weight,
    norm_gain,
    gate_weight,
    up_weight,
    down_weight,
):
    pools = lax.axis_size("pool")
    amount = queries.shape[0]
    pad = -(-amount // PAD) * PAD
    attended = attend(queries, cached_entries, new_entry, lengths)
    att = attended.reshape(amount, pools, -1).transpose(1, 0, 2)
    att = jnp.pad(att, ((0, 0), (0, pad - amount), (0, 0)))
    return finish_rows(
        att,
        residual,
        norm_gain.astype(jnp.float32)[None, :],
        out_weight,
        gate_weight,
        up_weight,
        down_weight,
        amount,
    )


def solution(mesh):
    placed = (
        P(("groups", "pool", "tp"), None),
        P(("groups", "pool", "tp"), None, None),
        P(("groups", "pool", "tp"), None),
        P(("groups", "pool", "tp")),
        P(("groups", "pool"), "tp"),
        P("pool", "tp"),
        P("tp"),
        P("tp", "pool"),
        P("tp", "pool"),
        P("pool", "tp"),
    )
    return jax.shard_map(
        on_device,
        mesh=mesh,
        in_specs=placed,
        out_specs=P(("groups", "pool"), "tp"),
        check_vma=False,
    )
```
